32 devices in a mesh: expert: 8 (over z, x), hidden: 4 (over y, core).
Axes of the slice: x: 2, y: 2, z: 4, core: 2. Of those that a mesh axis runs over, the one named last changes fastest.
Arguments:
- tokens: bfloat16 [768, 4096], P('expert', 'hidden'), may hold values from -6 to 6
- gate_weight: bfloat16 [16, 4096, 1536], P('expert', None, 'hidden'), may hold values from -0.09375 to 0.09375
- up_weight: bfloat16 [16, 4096, 1536], P('expert', None, 'hidden'), may hold values from -0.09375 to 0.09375
- down_weight: bfloat16 [16, 1536, 4096], P('expert', 'hidden'), may hold values from -0.15625 to 0.15625
- swap_slot: int32 [8], replicated, may hold values from 0 to 1
- expert_ids: int32 [768, 8], P('expert'), may hold values from 0 to 15, as said below
- gate_fixed: int32 [768, 8], P('expert'), may hold values from 1 to 65535
Outputs:
- moe_out: bfloat16 [768, 4096], P('expert', 'hidden')
The draws below stay inside these ranges and needn't reach their ends.
Inputs may be any that keep to these rules, and one draw needn't show every extreme that they name: `expert_ids`: each row names 8 ids on 8 different indices of the expert axis (index = id // 2). In the 96 rows of each index of the expert axis, every index is named exactly 96 times.
All inputs are finite; a program needn't handle non-finite values.
Results may differ from the reference program's by a relative error of at most 0.012.
Values may be sent and summed in bfloat16 or wider, within the bound.
A program may use at most 192 MiB of HBM per device.

```python
import jax
import jax.numpy as jnp
from jax import lax

D = 4096
FF = 1536
TOPK = 8
EXP_DEV = 2
TOK_DEV = 96
EXPERTS = 16
TOKENS = 768
N_EXPERT = 8
N_HIDDEN = 4


def draw_expert_ids(key, part):
    subkeys = jax.random.split(key, 2)

    def one_block(block_num):
        shuffled = jax.random.permutation(jax.random.fold_in(subkeys[0], block_num), N_EXPERT)
        position = (jnp.arange(TOK_DEV)[:, None] * TOPK + jnp.arange(TOPK)[None, :]) % N_EXPERT
        return shuffled[position]
    devices = jax.vmap(one_block)(jnp.arange(N_EXPERT)).reshape(TOKENS, TOPK)
    slots = jax.random.randint(subkeys[1], (TOKENS, TOPK), 0, EXP_DEV)
    return (devices * EXP_DEV + slots).astype(jnp.int32)


def place_ends(drawn, stream_key, smallest, largest):
    spot = [jax.random.randint(jax.random.fold_in(stream_key, axis), (), 0, length) for axis, length in enumerate(drawn.shape)]
    widest = drawn.shape.index(max(drawn.shape))
    beside = spot[:widest] + [(spot[widest] + 1) % drawn.shape[widest]] + spot[widest + 1:]
    return drawn.at[tuple(spot)].set(smallest).at[tuple(beside)].set(largest)


def steps_of(stream_key, extent, cuts, low, largest):
    level, own = 1.0, jax.random.fold_in(stream_key, 6)
    for dim, blocks in cuts:
        heights = jnp.exp(jax.random.uniform(jax.random.fold_in(own, dim), (blocks,), jnp.float32, low / len(cuts), largest / len(cuts)))
        level = level * jnp.repeat(heights, extent[dim] // blocks).reshape([-1 if axis == dim else 1 for axis in range(len(extent))])
    return level


def gaussian(stream_key, shape, spread, bound, shards=(), held_as=jnp.bfloat16):
    result = spread * jax.random.normal(stream_key, shape, jnp.float32)
    if shards:
        result = result * steps_of(stream_key, shape, shards, -0.22, 0.18)
    return jnp.clip(result, -bound, bound).astype(held_as)


def setup_inputs(seed: int = 0) -> dict:
    splits = jax.random.split(jax.random.key(seed), 8)
    return {
        "tokens": gaussian(splits[0], (TOKENS, D), 1.0, 6.0, ((0, 8), (1, 4))),
        "gate_weight": gaussian(splits[1], (EXPERTS, D, FF), D ** -0.5, 0.09375, ((0, 8), (2, 4))),
        "up_weight": gaussian(splits[2], (EXPERTS, D, FF), D ** -0.5, 0.09375, ((0, 8), (2, 4))),
        "down_weight": gaussian(splits[3], (EXPERTS, FF, D), FF ** -0.5, 0.15625, ((0, 8), (1, 4))),
        "swap_slot": place_ends(jax.random.randint(splits[4], (N_EXPERT,), 0, EXP_DEV), jax.random.fold_in(splits[4], 1), 0, EXP_DEV - 1).astype(jnp.int32),
        "expert_ids": draw_expert_ids(jax.random.fold_in(splits[7], 71), 0),
        "gate_fixed": place_ends(jax.random.randint(splits[6], (TOKENS, TOPK), 1, 65536), jax.random.fold_in(splits[6], 1), 1, 65535).astype(jnp.int32),
    }


def reference(tokens, gate_weight, up_weight, down_weight, swap_slot, expert_ids, gate_fixed):
    scores = gate_fixed.astype(jnp.float32)
    gate_norm = scores / jnp.sum(scores, axis=1, keepdims=True)
    half_axis = N_EXPERT // 2
    device_of = (expert_ids // EXP_DEV).astype(jnp.int32)
    slot_local = (expert_ids % EXP_DEV).astype(jnp.int32)
    partner = ((device_of + half_axis) % N_EXPERT).astype(jnp.int32)
    is_moved = slot_local == swap_slot[device_of]
    source_id = jnp.where(is_moved, partner * EXP_DEV + swap_slot[partner], expert_ids).astype(jnp.int32)
    flat_anchor = source_id.reshape(-1)
    flat_weight = gate_norm.reshape(-1)
    token_of = (jnp.arange(TOKENS * TOPK) // TOPK).astype(jnp.int32)
    capacity = TOPK * TOK_DEV
    quarter = FF // N_HIDDEN

    def one_expert(result_rows, expert_id):
        member = flat_anchor == expert_id
        picked = jnp.argsort(jnp.where(member, 0, 1).astype(jnp.int32), stable=True)[:capacity]
        is_member = member[picked]
        row_index = token_of[picked]
        row_block = tokens[row_index]
        gate_out = jnp.dot(row_block, gate_weight[expert_id], preferred_element_type=jnp.float32)
        up_out = jnp.dot(row_block, up_weight[expert_id], preferred_element_type=jnp.float32)
        hidden = (jax.nn.silu(gate_out) * up_out).astype(jnp.bfloat16)
        accum_rows = jnp.zeros((capacity, D), jnp.float32)
        for quarter_idx in range(N_HIDDEN):
            lower = quarter_idx * quarter
            quarter_out = jnp.dot(hidden[:, lower:lower + quarter], down_weight[expert_id, lower:lower + quarter], preferred_element_type=jnp.float32).astype(jnp.bfloat16)
            quarter_out = lax.optimization_barrier(quarter_out)
            accum_rows = accum_rows + quarter_out.astype(jnp.float32)
        pair_weight = jnp.where(is_member, flat_weight[picked], jnp.float32(0.0))
        result_rows = result_rows.at[row_index].add(accum_rows * pair_weight[:, None])
        return result_rows, None

    result_rows, _ = lax.scan(one_expert, jnp.zeros((TOKENS, D), jnp.float32), jnp.arange(EXPERTS, dtype=jnp.int32))
    return result_rows.astype(jnp.bfloat16)
```

```python
import jax
import jax.numpy as jnp
from jax import lax
from jax.sharding import PartitionSpec as P


def slot_weights(expert_ids, gate_fixed, swap_slot, slots_here):
    axis_count = lax.axis_size("expert")
    me = lax.axis_index("expert")
    scores = gate_fixed.astype(jnp.float32)
    gate_norm = scores / jnp.sum(scores, axis=1, keepdims=True)
    home = expert_ids // slots_here
    slot = expert_ids % slots_here
    onehot = home[:, :, None] == jnp.arange(axis_count, dtype=jnp.int32)
    own_swap = jnp.sum(jnp.where(onehot, swap_slot, 0), axis=2)
    other_swap = jnp.sum(jnp.where(onehot, jnp.roll(swap_slot, -(axis_count // 2)), 0), axis=2)
    other = (home + axis_count // 2) % axis_count
    source = jnp.where(slot == own_swap, other * slots_here + other_swap, expert_ids)
    mine = me * slots_here + jnp.arange(slots_here, dtype=jnp.int32)
    return jnp.sum(jnp.where(source[:, :, None] == mine, gate_norm[:, :, None], 0.0), axis=1)


def per_device(tokens, gate_weight, up_weight, down_weight, swap_slot, expert_ids, gate_fixed):
    slots_here = gate_weight.shape[0]
    ids_all = lax.all_gather(expert_ids, "expert", axis=0, tiled=True)
    gates_all = lax.all_gather(gate_fixed, "expert", axis=0, tiled=True)
    weight = slot_weights(ids_all, gates_all, swap_slot, slots_here)
    rows = lax.all_gather(tokens, "hidden", axis=1, tiled=True)
    rows = lax.all_gather(rows, "expert", axis=0, tiled=True)
    total = None
    for s in range(slots_here):
        gate_out = jnp.dot(rows, gate_weight[s], preferred_element_type=jnp.float32)
        up_out = jnp.dot(rows, up_weight[s], preferred_element_type=jnp.float32)
        hidden = (jax.nn.silu(gate_out) * up_out * weight[:, s : s + 1]).astype(jnp.bfloat16)
        out = jnp.dot(hidden, down_weight[s], preferred_element_type=jnp.float32)
        total = out if total is None else total + out
    total = total.astype(jnp.bfloat16)
    part = lax.psum_scatter(total, "expert", scatter_dimension=0, tiled=True)
    return lax.psum_scatter(part, "hidden", scatter_dimension=1, tiled=True)


def solution(mesh):
    in_specs = (
        P("expert", "hidden"),
        P("expert", None, "hidden"),
        P("expert", None, "hidden"),
        P("expert", "hidden", None),
        P(),
        P("expert", None),
        P("expert", None),
    )
    return jax.shard_map(
        per_device, mesh=mesh, in_specs=in_specs, out_specs=P("expert", "hidden"), check_vma=False
    )
```

```python
import jax
import jax.numpy as jnp
from jax import lax
from jax.experimental import pallas as pl
from jax.experimental.pallas import tpu as pltpu
from jax.sharding import PartitionSpec as P

MESH = pl.DeviceIdType.MESH
F32 = jnp.float32
BF16 = jnp.bfloat16


def slot_weights(expert_ids, gate_fixed, swap_slot, slots_here):
    axis_count = lax.axis_size("expert")
    me = lax.axis_index("expert")
    scores = gate_fixed.astype(jnp.float32)
    gate_norm = scores / jnp.sum(scores, axis=1, keepdims=True)
    home = expert_ids // slots_here
    slot = expert_ids % slots_here
    onehot = home[:, :, None] == jnp.arange(axis_count, dtype=jnp.int32)
    own_swap = jnp.sum(jnp.where(onehot, swap_slot, 0), axis=2)
    other_swap = jnp.sum(jnp.where(onehot, jnp.roll(swap_slot, -(axis_count // 2)), 0), axis=2)
    other = (home + axis_count // 2) % axis_count
    source = jnp.where(slot == own_swap, other * slots_here + other_swap, expert_ids)
    mine = me * slots_here + jnp.arange(slots_here, dtype=jnp.int32)
    return jnp.sum(jnp.where(source[:, :, None] == mine, gate_norm[:, :, None], 0.0), axis=1)


def dense_device(tokens, gate_weight, up_weight, down_weight, swap_slot, expert_ids, gate_fixed):
    slots_here = gate_weight.shape[0]
    ids_all = lax.all_gather(expert_ids, "expert", axis=0, tiled=True)
    gates_all = lax.all_gather(gate_fixed, "expert", axis=0, tiled=True)
    weight = slot_weights(ids_all, gates_all, swap_slot, slots_here)
    rows = lax.all_gather(tokens, "hidden", axis=1, tiled=True)
    rows = lax.all_gather(rows, "expert", axis=0, tiled=True)
    total = None
    for s in range(slots_here):
        gate_out = jnp.dot(rows, gate_weight[s], preferred_element_type=jnp.float32)
        up_out = jnp.dot(rows, up_weight[s], preferred_element_type=jnp.float32)
        hidden = (jax.nn.silu(gate_out) * up_out * weight[:, s : s + 1]).astype(jnp.bfloat16)
        out = jnp.dot(hidden, down_weight[s], preferred_element_type=jnp.float32)
        total = out if total is None else total + out
    total = total.astype(jnp.bfloat16)
    part = lax.psum_scatter(total, "expert", scatter_dimension=0, tiled=True)
    return lax.psum_scatter(part, "hidden", scatter_dimension=1, tiled=True)


def fused_kernel(
    tok_ref, gate_ref, up_ref, down_ref, ids_ref, fix_ref, swap_ref, out_ref,
    buf, wgu, wd, hid, wcol, pbuf, wt, rs_sib, rs_sec, rs_fst, rs_z, own_sum,
    load_sem, ag_send, ag_recv, wt_send, wt_recv, rs_send, rs_recv,
):
    rows, cols = tok_ref.shape
    slots, width, ff = gate_ref.shape
    tiles = ff // 128
    e, h = lax.axis_index("expert"), lax.axis_index("hidden")
    z, x = lax.div(e, 2), lax.rem(e, 2)
    y, c = lax.div(h, 2), lax.rem(h, 2)
    zs = [z, z + 1 - 2 * lax.rem(z, 2), lax.rem(z + 2, 4), 3 - z]
    fx, fy = x + (1 - c) * (1 - 2 * x), y + c * (1 - 2 * y)
    sx, sy = x + c * (1 - 2 * x), y + (1 - c) * (1 - 2 * y)

    def dev(zz, xx, yy, cc):
        return (zz * 2 + xx, yy * 2 + cc)

    line = [dev(zs[k], x, y, c) for k in range(4)]
    cross = [dev(zs[k], 1 - x, y, c) for k in range(4)]
    first, second, sibling = dev(z, fx, fy, c), dev(z, sx, sy, c), dev(z, x, y, 1 - c)

    loads = []

    def load(source, target):
        copy = pltpu.make_async_copy(source, target, load_sem.at[len(loads)])
        copy.start()
        loads.append(copy)

    def row_slice(xx):
        return pl.ds(pl.multiple_of(xx * rows, 32), rows)

    def block(k, yy, xx, cc):
        return buf.at[k, yy * 2 + cc, row_slice(xx), :]

    load(tok_ref, block(0, y, x, c))
    for s in range(slots):
        for j in range(tiles):
            span = pl.ds(j * 128, 128)
            load(gate_ref.at[s, :, span], wgu.at[s * tiles + j, :, pl.ds(0, 128)])
            load(up_ref.at[s, :, span], wgu.at[s * tiles + j, :, pl.ds(128, 128)])
    for s in range(slots):
        load(down_ref.at[s], wd.at[pl.ds(s * ff, ff), :])

    ids = ids_ref[...]
    scores = fix_ref[...].astype(F32)
    gate_norm = scores / jnp.sum(scores, axis=1, keepdims=True)
    axis_count = swap_ref.shape[0]
    home = lax.div(ids, slots)
    own_swap = jnp.zeros_like(ids)
    other_swap = jnp.zeros_like(ids)
    for j in range(axis_count):
        own_swap = jnp.where(home == j, swap_ref[j], own_swap)
        other_swap = jnp.where(home == j, swap_ref[(j + axis_count // 2) % axis_count], other_swap)
    other = lax.rem(home + axis_count // 2, axis_count)
    source = jnp.where(ids - home * slots == own_swap, other * slots + other_swap, ids)
    lane = lax.broadcasted_iota(jnp.int32, (rows, 128), 1)
    table = jnp.zeros((rows, 128), F32)
    for k in range(ids.shape[1]):
        table = table + jnp.where(source[:, k : k + 1] == lane, gate_norm[:, k : k + 1], 0.0)
    table = jnp.concatenate([table, jnp.zeros((128 - rows, 128), F32)], axis=0)
    wt[0, x] = jnp.transpose(table)[: wt.shape[2]]

    barrier = pltpu.get_barrier_semaphore()
    peers = line[1:] + cross[1:] + [first, second, sibling]
    for peer in peers:
        pl.semaphore_signal(barrier, inc=1, device_id=peer, device_id_type=MESH)
    pl.semaphore_wait(barrier, len(peers))

    started = []

    def remote(source, target, sends, recvs, i, peer):
        return pltpu.make_async_remote_copy(
            src_ref=source, dst_ref=target, send_sem=sends.at[i], recv_sem=recvs.at[i],
            device_id=peer, device_id_type=MESH,
        )

    def send(*what):
        copy = remote(*what)
        copy.start()
        started.append(copy)

    def gather(i, source, target, peer):
        send(source, target, ag_send, ag_recv, i, peer)

    def arrived(i, target, peer):
        remote(target, target, ag_send, ag_recv, i, peer).wait_recv()

    def base(k):
        return 3 + 7 * k

    def a0(k):
        if k > 3:
            return
        mine = block(k, y, x, c)
        if k:
            arrived(k - 1, mine, line[k])
        gather(base(k), mine, mine, first)
        gather(base(k) + 1, mine, mine, second)
        gather(base(k) + 3, mine, mine, sibling)

    def a1(k):
        if k > 3:
            return
        got = block(k, fy, fx, c)
        arrived(base(k), got, first)
        gather(base(k) + 2, got, got, second)
        gather(base(k) + 4, got, got, sibling)

    def a2(k):
        if k > 3:
            return
        for n, got in enumerate([block(k, sy, sx, c), block(k, 1 - y, 1 - x, c)]):
            arrived(base(k) + 1 + n, got, second)
            gather(base(k) + 5 + n, got, got, sibling)

    def a3(k):
        if k > 3:
            return
        for n, (yy, xx) in enumerate([(y, x), (sy, sx), (fy, fx), (1 - y, 1 - x)]):
            arrived(base(k) + 3 + n, block(k, yy, xx, 1 - c), sibling)

    a_me, b_me = y + c * (x - y), x + c * (y - x)

    def scatter(i, source, target, peer):
        send(source, target, rs_send, rs_recv, i, peer)

    def summed(i, target, peer):
        remote(target, target, rs_send, rs_recv, i, peer).wait_recv()

    def r0(k):
        scatter(4 * k, pbuf.at[k, 1 - c], rs_sib.at[k], sibling)

    def r1(k):
        if k < 0:
            return
        summed(4 * k, rs_sib.at[k], sibling)
        away = 1 - a_me
        pbuf[k, c, away] = (pbuf[k, c, away].astype(F32) + rs_sib[k, away].astype(F32)).astype(BF16)
        scatter(4 * k + 1, pbuf.at[k, c, away], rs_sec.at[k], second)
        pbuf[k, c, a_me] = (pbuf[k, c, a_me].astype(F32) + rs_sib[k, a_me].astype(F32)).astype(BF16)

    def r2(k):
        if k < 0:
            return
        summed(4 * k + 1, rs_sec.at[k], second)
        away = 1 - b_me
        pbuf[k, c, a_me, away] = (
            pbuf[k, c, a_me, away].astype(F32) + rs_sec[k, away].astype(F32)
        ).astype(BF16)
        scatter(4 * k + 2, pbuf.at[k, c, a_me, away], rs_fst.at[k], first)

    def r3(k):
        if k < 0:
            return
        summed(4 * k + 2, rs_fst.at[k], first)
        total = (
            pbuf[k, c, a_me, b_me].astype(F32)
            + rs_sec[k, b_me].astype(F32)
            + rs_fst[k].astype(F32)
        )
        if k:
            pbuf[k, c, a_me, b_me] = total.astype(BF16)
            scatter(4 * k + 3, pbuf.at[k, c, a_me, b_me], rs_z.at[k - 1], line[k])
        else:
            own_sum[...] = total

    def weight_columns(k):
        for xx in range(2):
            part = wt[k, xx]
            sub = lax.broadcasted_iota(jnp.int32, part.shape, 0)
            for s in range(slots):
                row = jnp.sum(jnp.where(sub == e * slots + s, part, 0.0), axis=0, keepdims=True)
                column = jnp.transpose(jnp.broadcast_to(row, (128, 128)))
                wcol[s, xx * rows : (xx + 1) * rows, :] = column[:rows]

    def up_gate(k, s):
        @pl.loop(0, tiles)
        def _(j):
            acc = jnp.zeros((2 * rows, 256), F32)
            for q in range(buf.shape[1]):
                acc = acc + jnp.dot(
                    buf[k, q], wgu[s * tiles + j, q * cols : (q + 1) * cols, :],
                    preferred_element_type=F32,
                )
            gate_out, up_out = acc[:, :128], acc[:, 128:]
            value = gate_out / (1.0 + jnp.exp(-gate_out)) * up_out * wcol[s]
            hid[:, pl.ds(pl.multiple_of(s * ff + j * 128, 128), 128)] = value.astype(BF16)

    def down(k):
        for q in range(buf.shape[1]):
            out = jnp.dot(hid[...], wd[:, q * cols : (q + 1) * cols], preferred_element_type=F32)
            out = out.astype(BF16)
            yy, cc = q // 2, q % 2
            for xx in range(2):
                a, b = (yy, xx) if cc == 0 else (xx, yy)
                pbuf[k, cc, a, b] = out[xx * rows : (xx + 1) * rows]

    loads[0].wait()
    gather_own = block(0, y, x, c)
    a0(0)
    for k in (1, 2, 3):
        gather(k - 1, gather_own, block(k, y, x, c), line[k])
    tags = [(line[1], 1, 0), (line[2], 2, 1), (line[3], 3, 2)]
    tags += [(cross[k], k, 3 + k) for k in range(4)]
    for peer, k, i in tags:
        send(wt.at[0, x], wt.at[k, x], wt_send, wt_recv, i, peer)
    a1(0)
    a0(1)
    a2(0)
    a1(1)
    for peer, k, i in tags:
        got = wt.at[k, x if i < 3 else 1 - x]
        remote(got, got, wt_send, wt_recv, i, peer).wait_recv()
    a0(2)
    for copy in loads[1:]:
        copy.wait()
    a3(0)
    for k in range(4):
        weight_columns(k)
        up_gate(k, 0)
        a2(k + 1)
        a1(k + 2)
        r1(k - 1)
        up_gate(k, 1)
        a0(k + 3)
        r2(k - 1)
        down(k)
        r0(k)
        r3(k - 1)
        a3(k + 1)
    r1(3)
    r2(3)
    r3(3)
    total = own_sum[...]
    for k in (1, 2, 3):
        summed(4 * k + 3, rs_z.at[k - 1], line[k])
        total = total + rs_z[k - 1].astype(F32)
    out_ref[...] = total.astype(BF16)
    for copy in started:
        copy.wait_send()


def fused_device(tokens, gate_weight, up_weight, down_weight, swap_slot, expert_ids, gate_fixed):
    rows, cols = tokens.shape
    slots, width, ff = gate_weight.shape
    quarters = width // cols
    chunks = 4
    scratch = [
        pltpu.VMEM((chunks, quarters, 2 * rows, cols), BF16),
        pltpu.VMEM((slots * ff // 128, width, 256), BF16),
        pltpu.VMEM((slots * ff, width), BF16),
        pltpu.VMEM((2 * rows, slots * ff), BF16),
        pltpu.VMEM((slots, 2 * rows, 128), F32),
        pltpu.VMEM((chunks, 2, 2, 2, rows, cols), BF16),
        pltpu.VMEM((chunks, 2, 16, 128), F32),
        pltpu.VMEM((chunks, 2, 2, rows, cols), BF16),
        pltpu.VMEM((chunks, 2, rows, cols), BF16),
        pltpu.VMEM((chunks, rows, cols), BF16),
        pltpu.VMEM((chunks - 1, rows, cols), BF16),
        pltpu.VMEM((rows, cols), F32),
        pltpu.SemaphoreType.DMA((1 + 2 * slots * (ff // 128) + slots,)),
        pltpu.SemaphoreType.DMA((3 + 7 * chunks,)),
        pltpu.SemaphoreType.DMA((3 + 7 * chunks,)),
        pltpu.SemaphoreType.DMA((7,)),
        pltpu.SemaphoreType.DMA((7,)),
        pltpu.SemaphoreType.DMA((4 * chunks,)),
        pltpu.SemaphoreType.DMA((4 * chunks,)),
    ]
    any_space = pl.BlockSpec(memory_space=pl.ANY)
    vmem = pl.BlockSpec(memory_space=pltpu.VMEM)
    return pl.pallas_call(
        fused_kernel,
        out_shape=jax.ShapeDtypeStruct((rows, cols), BF16),
        in_specs=[any_space] * 4 + [vmem, vmem, pl.BlockSpec(memory_space=pltpu.SMEM)],
        out_specs=vmem,
        scratch_shapes=scratch,
        compiler_params=pltpu.CompilerParams(
            collective_id=0, has_side_effects=True, vmem_limit_bytes=56 * 1024 * 1024
        ),
    )(tokens, gate_weight, up_weight, down_weight, expert_ids, gate_fixed, swap_slot)


def per_device(tokens, *rest):
    small = lax.axis_size("expert") == 8 and lax.axis_size("hidden") == 4
    fits = tokens.shape == (96, 1024) and rest[0].shape == (2, 4096, 384)
    return fused_device(tokens, *rest) if small and fits else dense_device(tokens, *rest)


def solution(mesh):
    in_specs = (
        P("expert", "hidden"),
        P("expert", None, "hidden"),
        P("expert", None, "hidden"),
        P("expert", "hidden", None),
        P(),
        P("expert", None),
        P("expert", None),
    )
    return jax.shard_map(
        per_device, mesh=mesh, in_specs=in_specs, out_specs=P("expert", "hidden"), check_vma=False
    )
```

```python
import jax
import jax.numpy as jnp
from jax import lax
from jax.experimental import pallas as pl
from jax.experimental.pallas import tpu as pltpu
from jax.sharding import PartitionSpec as P

MESH = pl.DeviceIdType.MESH
F32 = jnp.float32
BF16 = jnp.bfloat16


def slot_weights(expert_ids, gate_fixed, swap_slot, slots_here):
    axis_count = lax.axis_size("expert")
    me = lax.axis_index("expert")
    scores = gate_fixed.astype(jnp.float32)
    gate_norm = scores / jnp.sum(scores, axis=1, keepdims=True)
    home = expert_ids // slots_here
    slot = expert_ids % slots_here
    onehot = home[:, :, None] == jnp.arange(axis_count, dtype=jnp.int32)
    own_swap = jnp.sum(jnp.where(onehot, swap_slot, 0), axis=2)
    other_swap = jnp.sum(jnp.where(onehot, jnp.roll(swap_slot, -(axis_count // 2)), 0), axis=2)
    other = (home + axis_count // 2) % axis_count
    source = jnp.where(slot == own_swap, other * slots_here + other_swap, expert_ids)
    mine = me * slots_here + jnp.arange(slots_here, dtype=jnp.int32)
    return jnp.sum(jnp.where(source[:, :, None] == mine, gate_norm[:, :, None], 0.0), axis=1)


def dense_device(tokens, gate_weight, up_weight, down_weight, swap_slot, expert_ids, gate_fixed):
    slots_here = gate_weight.shape[0]
    ids_all = lax.all_gather(expert_ids, "expert", axis=0, tiled=True)
    gates_all = lax.all_gather(gate_fixed, "expert", axis=0, tiled=True)
    weight = slot_weights(ids_all, gates_all, swap_slot, slots_here)
    rows = lax.all_gather(tokens, "hidden", axis=1, tiled=True)
    rows = lax.all_gather(rows, "expert", axis=0, tiled=True)
    total = None
    for s in range(slots_here):
        gate_out = jnp.dot(rows, gate_weight[s], preferred_element_type=jnp.float32)
        up_out = jnp.dot(rows, up_weight[s], preferred_element_type=jnp.float32)
        hidden = (jax.nn.silu(gate_out) * up_out * weight[:, s : s + 1]).astype(jnp.bfloat16)
        out = jnp.dot(hidden, down_weight[s], preferred_element_type=jnp.float32)
        total = out if total is None else total + out
    total = total.astype(jnp.bfloat16)
    part = lax.psum_scatter(total, "expert", scatter_dimension=0, tiled=True)
    return lax.psum_scatter(part, "hidden", scatter_dimension=1, tiled=True)


def fused_kernel(
    tok_ref, gate_ref, up_ref, down_ref, ids_ref, fix_ref, swap_ref, out_ref,
    buf, wgu, wd, hid, wcol, pbuf, wt, rs_sib, rs_sec, rs_fst, rs_z, own_sum,
    load_sem, ag_send, ag_recv, wt_send, wt_recv, rs_send, rs_recv,
):
    rows, cols = tok_ref.shape
    slots, width, ff = gate_ref.shape
    tiles = ff // 128
    e, h = lax.axis_index("expert"), lax.axis_index("hidden")
    z, x = lax.div(e, 2), lax.rem(e, 2)
    y, c = lax.div(h, 2), lax.rem(h, 2)
    zs = [z, z + 1 - 2 * lax.rem(z, 2), lax.rem(z + 2, 4), 3 - z]
    halves = (0, 1)
    half = cols // 2
    f_at, s_at = [(y, 1 - x), (1 - y, x)], [(1 - y, x), (y, 1 - x)]

    def dev(zz, xx, yy, cc):
        return (zz * 2 + xx, yy * 2 + cc)

    line = [dev(zs[k], x, y, c) for k in range(4)]
    cross = [dev(zs[k], 1 - x, y, c) for k in range(4)]
    firsts = [dev(z, 1 - x, y, c), dev(z, x, 1 - y, c)]
    seconds = firsts[::-1]
    sibling = dev(z, x, y, 1 - c)

    loads = []

    def load(source, target):
        copy = pltpu.make_async_copy(source, target, load_sem.at[len(loads)])
        copy.start()
        loads.append(copy)

    def row_slice(xx):
        return pl.ds(pl.multiple_of(xx * rows, 32), rows)

    def block(k, at, cc, p=None):
        span = slice(None) if p is None else pl.ds(p * half, half)
        return buf.at[k, at[0] * 2 + cc, row_slice(at[1]), span]

    load(tok_ref, block(0, (y, x), c))

    barrier = pltpu.get_barrier_semaphore()
    peers = line[1:] + cross[1:] + firsts + [sibling]
    for peer in peers:
        pl.semaphore_signal(barrier, inc=1, device_id=peer, device_id_type=MESH)

    ids = ids_ref[...]
    scores = fix_ref[...].astype(F32)
    gate_norm = scores / jnp.sum(scores, axis=0, keepdims=True)
    axis_count = swap_ref.shape[0]
    home = lax.div(ids, slots)
    own_swap = jnp.zeros_like(ids)
    other_swap = jnp.zeros_like(ids)
    for j in range(axis_count):
        own_swap = jnp.where(home == j, swap_ref[j], own_swap)
        other_swap = jnp.where(home == j, swap_ref[(j + axis_count // 2) % axis_count], other_swap)
    other = lax.rem(home + axis_count // 2, axis_count)
    source = jnp.where(ids - home * slots == own_swap, other * slots + other_swap, ids)
    experts = wt.shape[2]
    sub = lax.broadcasted_iota(jnp.int32, (experts, rows), 0)
    table = jnp.zeros((experts, rows), F32)
    for k in range(ids.shape[0]):
        table = table + jnp.where(source[k : k + 1, :] == sub, gate_norm[k : k + 1, :], 0.0)
    wt[0, x] = jnp.zeros((experts, 128), F32)
    wt[0, x, :, 0:rows] = table

    started = []

    def remote(source, target, sends, recvs, i, peer):
        return pltpu.make_async_remote_copy(
            src_ref=source, dst_ref=target, send_sem=sends.at[i], recv_sem=recvs.at[i],
            device_id=peer, device_id_type=MESH,
        )

    def send(*what):
        copy = remote(*what)
        copy.start()
        started.append(copy)

    def gather(i, source, target, peer):
        send(source, target, ag_send, ag_recv, i, peer)

    def arrived(i, target, peer):
        remote(target, target, ag_send, ag_recv, i, peer).wait_recv()

    def base(k):
        return 3 + 13 * k

    def a0(k):
        if k > 3:
            return
        mine = block(k, (y, x), c)
        if k:
            arrived(k - 1, mine, line[k])
        for p in halves:
            part = block(k, (y, x), c, p)
            gather(base(k) + 3 * p, part, part, firsts[p])
        for p in halves:
            part = block(k, (y, x), c, p)
            gather(base(k) + 3 * p + 1, part, part, seconds[p])
        gather(base(k) + 6, mine, mine, sibling)

    def a1(k):
        if k > 3:
            return
        for p in halves:
            got = block(k, f_at[p], c, p)
            arrived(base(k) + 3 * p, got, firsts[p])
            gather(base(k) + 3 * p + 2, got, got, seconds[p])
            gather(base(k) + 7 + p, got, got, sibling)

    def second_blocks(k, cc):
        return [
            (2 * p + n, block(k, at, cc, p), seconds[p])
            for n in (0, 1)
            for p, at in enumerate(s_at if n == 0 else [(1 - y, 1 - x)] * 2)
        ]

    def a2(k):
        if k > 3:
            return
        for i, got, peer in second_blocks(k, c):
            arrived(base(k) + 3 * (i // 2) + 1 + i % 2, got, peer)
            gather(base(k) + 9 + i, got, got, sibling)

    def a3(k):
        if k > 3:
            return
        arrived(base(k) + 6, block(k, (y, x), 1 - c), sibling)
        for p in halves:
            arrived(base(k) + 7 + p, block(k, f_at[p], 1 - c, p), sibling)
        for i, got, _ in second_blocks(k, 1 - c):
            arrived(base(k) + 9 + i, got, sibling)

    a_me, b_me = [y, x], [x, y]

    def scatter(i, source, target, peer):
        send(source, target, rs_send, rs_recv, i, peer)

    def summed(i, target, peer):
        remote(target, target, rs_send, rs_recv, i, peer).wait_recv()

    def add(k, p, a, b, other):
        pbuf[k, c, p, a, b] = (pbuf[k, c, p, a, b].astype(F32) + other.astype(F32)).astype(BF16)

    def r0(k):
        scatter(7 * k, pbuf.at[k, 1 - c], rs_sib.at[k], sibling)

    def r1(k):
        if k < 0:
            return
        summed(7 * k, rs_sib.at[k], sibling)
        for p in halves:
            away = 1 - a_me[p]
            for b in (0, 1):
                add(k, p, away, b, rs_sib[k, p, away, b])
            scatter(7 * k + 1 + p, pbuf.at[k, c, p, away], rs_sec.at[k, p], seconds[p])
        for p in halves:
            for b in (0, 1):
                add(k, p, a_me[p], b, rs_sib[k, p, a_me[p], b])

    def r2(k):
        if k < 0:
            return
        for p in halves:
            summed(7 * k + 1 + p, rs_sec.at[k, p], seconds[p])
            away = 1 - b_me[p]
            add(k, p, a_me[p], away, rs_sec[k, p, away])
            scatter(7 * k + 3 + p, pbuf.at[k, c, p, a_me[p], away], rs_fst.at[k, p], firsts[p])

    def r3(k):
        if k < 0:
            return
        for p in halves:
            summed(7 * k + 3 + p, rs_fst.at[k, p], firsts[p])
            total = (
                pbuf[k, c, p, a_me[p], b_me[p]].astype(F32)
                + rs_sec[k, p, b_me[p]].astype(F32)
                + rs_fst[k, p].astype(F32)
            )
            if k:
                pbuf[k, c, p, a_me[p], b_me[p]] = total.astype(BF16)
                mine = pbuf.at[k, c, p, a_me[p], b_me[p]]
                scatter(7 * k + 5 + p, mine, rs_z.at[k - 1, p], line[k])
            else:
                own_sum[p] = total

    def weight_columns(k):
        for xx in range(2):
            part = wt[k, xx]
            sub = lax.broadcasted_iota(jnp.int32, part.shape, 0)
            for s in range(slots):
                row = jnp.sum(jnp.where(sub == e * slots + s, part, 0.0), axis=0, keepdims=True)
                column = jnp.transpose(jnp.broadcast_to(row, (128, 128)))
                wcol[s, xx * rows : (xx + 1) * rows, :] = column[:rows]

    def up_gate(k, s):
        @pl.loop(0, tiles)
        def _(j):
            acc = jnp.zeros((2 * rows, 256), F32)
            for q in range(buf.shape[1]):
                acc = acc + jnp.dot(
                    buf[k, q], wgu[s * tiles + j, q * cols : (q + 1) * cols, :],
                    preferred_element_type=F32,
                )
            gate_out, up_out = acc[:, :128], acc[:, 128:]
            value = gate_out / (1.0 + jnp.exp(-gate_out)) * up_out * wcol[s]
            hid[:, pl.ds(pl.multiple_of(s * ff + j * 128, 128), 128)] = value.astype(BF16)

    def down(k):
        for q in range(buf.shape[1]):
            out = jnp.dot(hid[...], wd[:, q * cols : (q + 1) * cols], preferred_element_type=F32)
            out = out.astype(BF16)
            yy, cc = q // 2, q % 2
            for p in halves:
                for xx in range(2):
                    a, b = (yy, xx) if p == 0 else (xx, yy)
                    pbuf[k, cc, p, a, b] = out[
                        xx * rows : (xx + 1) * rows, p * half : (p + 1) * half
                    ]

    pl.semaphore_wait(barrier, len(peers))
    loads[0].wait()
    own = block(0, (y, x), c)
    a0(0)
    for k in (1, 2, 3):
        gather(k - 1, own, block(k, (y, x), c), line[k])
    tags = [(line[1], 1, 0), (line[2], 2, 1), (line[3], 3, 2)]
    tags += [(cross[k], k, 3 + k) for k in range(4)]
    for peer, k, i in tags:
        send(wt.at[0, x], wt.at[k, x], wt_send, wt_recv, i, peer)
    for s in range(slots):
        for j in range(tiles):
            span = pl.ds(j * 128, 128)
            load(gate_ref.at[s, :, span], wgu.at[s * tiles + j, :, pl.ds(0, 128)])
            load(up_ref.at[s, :, span], wgu.at[s * tiles + j, :, pl.ds(128, 128)])
    for s in range(slots):
        load(down_ref.at[s], wd.at[pl.ds(s * ff, ff), :])
    a1(0)
    a0(1)
    a2(0)
    a1(1)
    a0(2)
    for peer, k, i in tags:
        got = wt.at[k, x if i < 3 else 1 - x]
        remote(got, got, wt_send, wt_recv, i, peer).wait_recv()
    for copy in loads[1:]:
        copy.wait()
    a3(0)
    for k in range(4):
        weight_columns(k)
        up_gate(k, 0)
        a2(k + 1)
        a1(k + 2)
        r1(k - 1)
        r3(k - 2)
        up_gate(k, 1)
        a0(k + 3)
        down(k)
        r0(k)
        r2(k - 1)
        a3(k + 1)
    r1(3)
    r3(2)
    r2(3)
    r3(3)
    for p in halves:
        total = own_sum[p]
        for k in (1, 2, 3):
            summed(7 * k + 5 + p, rs_z.at[k - 1, p], line[k])
            total = total + rs_z[k - 1, p].astype(F32)
        out_ref[:, p * half : (p + 1) * half] = total.astype(BF16)
    for copy in started:
        copy.wait_send()


def fused_device(tokens, gate_weight, up_weight, down_weight, swap_slot, expert_ids, gate_fixed):
    rows, cols = tokens.shape
    slots, width, ff = gate_weight.shape
    quarters, half = width // cols, cols // 2
    chunks = 4
    scratch = [
        pltpu.VMEM((chunks, quarters, 2 * rows, cols), BF16),
        pltpu.VMEM((slots * ff // 128, width, 256), BF16),
        pltpu.VMEM((slots * ff, width), BF16),
        pltpu.VMEM((2 * rows, slots * ff), BF16),
        pltpu.VMEM((slots, 2 * rows, 128), F32),
        pltpu.VMEM((chunks, 2, 2, 2, 2, rows, half), BF16),
        pltpu.VMEM((chunks, 2, 16, 128), F32),
        pltpu.VMEM((chunks, 2, 2, 2, rows, half), BF16),
        pltpu.VMEM((chunks, 2, 2, rows, half), BF16),
        pltpu.VMEM((chunks, 2, rows, half), BF16),
        pltpu.VMEM((chunks - 1, 2, rows, half), BF16),
        pltpu.VMEM((2, rows, half), F32),
        pltpu.SemaphoreType.DMA((1 + 2 * slots * (ff // 128) + slots,)),
        pltpu.SemaphoreType.DMA((3 + 13 * chunks,)),
        pltpu.SemaphoreType.DMA((3 + 13 * chunks,)),
        pltpu.SemaphoreType.DMA((7,)),
        pltpu.SemaphoreType.DMA((7,)),
        pltpu.SemaphoreType.DMA((7 * chunks,)),
        pltpu.SemaphoreType.DMA((7 * chunks,)),
    ]
    any_space = pl.BlockSpec(memory_space=pl.ANY)
    vmem = pl.BlockSpec(memory_space=pltpu.VMEM)
    return pl.pallas_call(
        fused_kernel,
        out_shape=jax.ShapeDtypeStruct((rows, cols), BF16),
        in_specs=[any_space] * 4 + [vmem, vmem, pl.BlockSpec(memory_space=pltpu.SMEM)],
        out_specs=vmem,
        scratch_shapes=scratch,
        compiler_params=pltpu.CompilerParams(
            collective_id=0, has_side_effects=True, vmem_limit_bytes=56 * 1024 * 1024
        ),
    )(tokens, gate_weight, up_weight, down_weight, expert_ids.T, gate_fixed.T, swap_slot)


def per_device(tokens, *rest):
    small = lax.axis_size("expert") == 8 and lax.axis_size("hidden") == 4
    fits = tokens.shape == (96, 1024) and rest[0].shape == (2, 4096, 384)
    return fused_device(tokens, *rest) if small and fits else dense_device(tokens, *rest)


def solution(mesh):
    in_specs = (
        P("expert", "hidden"),
        P("expert", None, "hidden"),
        P("expert", None, "hidden"),
        P("expert", "hidden", None),
        P(),
        P("expert", None),
        P("expert", None),
    )
    return jax.shard_map(
        per_device, mesh=mesh, in_specs=in_specs, out_specs=P("expert", "hidden"), check_vma=False
    )
```

```python
import jax
import jax.numpy as jnp
from jax import lax
from jax.experimental import pallas as pl
from jax.experimental.pallas import tpu as pltpu
from jax.sharding import PartitionSpec as P

MESH = pl.DeviceIdType.MESH
F32 = jnp.float32
BF16 = jnp.bfloat16


def slot_weights(expert_ids, gate_fixed, swap_slot, slots_here):
    axis_count = lax.axis_size("expert")
    me = lax.axis_index("expert")
    scores = gate_fixed.astype(jnp.float32)
    gate_norm = scores / jnp.sum(scores, axis=1, keepdims=True)
    home = expert_ids // slots_here
    slot = expert_ids % slots_here
    onehot = home[:, :, None] == jnp.arange(axis_count, dtype=jnp.int32)
    own_swap = jnp.sum(jnp.where(onehot, swap_slot, 0), axis=2)
    other_swap = jnp.sum(jnp.where(onehot, jnp.roll(swap_slot, -(axis_count // 2)), 0), axis=2)
    other = (home + axis_count // 2) % axis_count
    source = jnp.where(slot == own_swap, other * slots_here + other_swap, expert_ids)
    mine = me * slots_here + jnp.arange(slots_here, dtype=jnp.int32)
    return jnp.sum(jnp.where(source[:, :, None] == mine, gate_norm[:, :, None], 0.0), axis=1)


def dense_device(tokens, gate_weight, up_weight, down_weight, swap_slot, expert_ids, gate_fixed):
    slots_here = gate_weight.shape[0]
    ids_all = lax.all_gather(expert_ids, "expert", axis=0, tiled=True)
    gates_all = lax.all_gather(gate_fixed, "expert", axis=0, tiled=True)
    weight = slot_weights(ids_all, gates_all, swap_slot, slots_here)
    rows = lax.all_gather(tokens, "hidden", axis=1, tiled=True)
    rows = lax.all_gather(rows, "expert", axis=0, tiled=True)
    total = None
    for s in range(slots_here):
        gate_out = jnp.dot(rows, gate_weight[s], preferred_element_type=jnp.float32)
        up_out = jnp.dot(rows, up_weight[s], preferred_element_type=jnp.float32)
        hidden = (jax.nn.silu(gate_out) * up_out * weight[:, s : s + 1]).astype(jnp.bfloat16)
        out = jnp.dot(hidden, down_weight[s], preferred_element_type=jnp.float32)
        total = out if total is None else total + out
    total = total.astype(jnp.bfloat16)
    part = lax.psum_scatter(total, "expert", scatter_dimension=0, tiled=True)
    return lax.psum_scatter(part, "hidden", scatter_dimension=1, tiled=True)


def fused_kernel(
    tok_ref, gate_ref, up_ref, down_ref, ids_ref, fix_ref, swap_ref, out_ref,
    buf, wgu, wd, hid, wcol, pbuf, wt, rs_sib, rs_sec, rs_fst, rs_z, own_sum,
    load_sem, ag_send, ag_recv, wt_send, wt_recv, rs_send, rs_recv,
):
    rows, cols = tok_ref.shape
    slots, width, ff = gate_ref.shape
    tiles = ff // 128
    e, h = lax.axis_index("expert"), lax.axis_index("hidden")
    z, x = lax.div(e, 2), lax.rem(e, 2)
    y, c = lax.div(h, 2), lax.rem(h, 2)
    zs = [z, z + 1 - 2 * lax.rem(z, 2), lax.rem(z + 2, 4), 3 - z]
    halves = (0, 1)
    half = cols // 2
    f_at, s_at = [(y, 1 - x), (1 - y, x)], [(1 - y, x), (y, 1 - x)]

    def dev(zz, xx, yy, cc):
        return (zz * 2 + xx, yy * 2 + cc)

    line = [dev(zs[k], x, y, c) for k in range(4)]
    cross = [dev(zs[k], 1 - x, y, c) for k in range(4)]
    firsts = [dev(z, 1 - x, y, c), dev(z, x, 1 - y, c)]
    seconds = firsts[::-1]
    sibling = dev(z, x, y, 1 - c)

    loads = []

    def load(source, target):
        copy = pltpu.make_async_copy(source, target, load_sem.at[len(loads)])
        copy.start()
        loads.append(copy)

    def row_slice(xx):
        return pl.ds(pl.multiple_of(xx * rows, 32), rows)

    def block(k, at, cc, p=None):
        span = slice(None) if p is None else pl.ds(p * half, half)
        return buf.at[k, at[0] * 2 + cc, row_slice(at[1]), span]

    load(tok_ref, block(0, (y, x), c))

    barrier = pltpu.get_barrier_semaphore()
    peers = line[1:] + cross[1:] + firsts + [sibling]
    for peer in peers:
        pl.semaphore_signal(barrier, inc=1, device_id=peer, device_id_type=MESH)

    ids = ids_ref[...]
    scores = fix_ref[...].astype(F32)
    gate_norm = scores / jnp.sum(scores, axis=0, keepdims=True)
    axis_count = swap_ref.shape[0]
    home = lax.div(ids, slots)
    own_swap = jnp.zeros_like(ids)
    other_swap = jnp.zeros_like(ids)
    for j in range(axis_count):
        own_swap = jnp.where(home == j, swap_ref[j], own_swap)
        other_swap = jnp.where(home == j, swap_ref[(j + axis_count // 2) % axis_count], other_swap)
    other = lax.rem(home + axis_count // 2, axis_count)
    source = jnp.where(ids - home * slots == own_swap, other * slots + other_swap, ids)
    experts = wt.shape[2]
    sub = lax.broadcasted_iota(jnp.int32, (experts, rows), 0)
    table = jnp.zeros((experts, rows), F32)
    for k in range(ids.shape[0]):
        table = table + jnp.where(source[k : k + 1, :] == sub, gate_norm[k : k + 1, :], 0.0)
    wt[0, x] = jnp.zeros((experts, 128), F32)
    wt[0, x, :, 0:rows] = table

    started = []

    def remote(source, target, sends, recvs, i, peer):
        return pltpu.make_async_remote_copy(
            src_ref=source, dst_ref=target, send_sem=sends.at[i], recv_sem=recvs.at[i],
            device_id=peer, device_id_type=MESH,
        )

    def send(*what):
        copy = remote(*what)
        copy.start()
        started.append(copy)

    def gather(i, source, target, peer):
        send(source, target, ag_send, ag_recv, i, peer)

    def arrived(i, target, peer):
        remote(target, target, ag_send, ag_recv, i, peer).wait_recv()

    def base(k):
        return 3 + 13 * k

    def a0(k):
        if k > 3:
            return
        mine = block(k, (y, x), c)
        if k:
            arrived(k - 1, mine, line[k])
        for p in halves:
            part = block(k, (y, x), c, p)
            gather(base(k) + 3 * p, part, part, firsts[p])
        for p in halves:
            part = block(k, (y, x), c, p)
            gather(base(k) + 3 * p + 1, part, part, seconds[p])
        gather(base(k) + 6, mine, mine, sibling)

    def a1(k):
        if k > 3:
            return
        for p in halves:
            got = block(k, f_at[p], c, p)
            arrived(base(k) + 3 * p, got, firsts[p])
            gather(base(k) + 3 * p + 2, got, got, seconds[p])
            gather(base(k) + 7 + p, got, got, sibling)

    def second_blocks(k, cc):
        return [
            (2 * p + n, block(k, at, cc, p), seconds[p])
            for n in (0, 1)
            for p, at in enumerate(s_at if n == 0 else [(1 - y, 1 - x)] * 2)
        ]

    def a2(k):
        if k > 3:
            return
        for i, got, peer in second_blocks(k, c):
            arrived(base(k) + 3 * (i // 2) + 1 + i % 2, got, peer)
            gather(base(k) + 9 + i, got, got, sibling)

    def a3(k):
        if k > 3:
            return
        arrived(base(k) + 6, block(k, (y, x), 1 - c), sibling)
        for p in halves:
            arrived(base(k) + 7 + p, block(k, f_at[p], 1 - c, p), sibling)
        for i, got, _ in second_blocks(k, 1 - c):
            arrived(base(k) + 9 + i, got, sibling)

    a_me, b_me = [y, x], [x, y]

    def scatter(i, source, target, peer):
        send(source, target, rs_send, rs_recv, i, peer)

    def summed(i, target, peer):
        remote(target, target, rs_send, rs_recv, i, peer).wait_recv()

    def add(k, p, a, b, other):
        pbuf[k, c, p, a, b] = (pbuf[k, c, p, a, b].astype(F32) + other.astype(F32)).astype(BF16)

    def r0(k):
        scatter(7 * k, pbuf.at[k, 1 - c], rs_sib.at[k], sibling)

    def r1(k):
        if k < 0:
            return
        summed(7 * k, rs_sib.at[k], sibling)
        for p in halves:
            away = 1 - a_me[p]
            for b in (0, 1):
                add(k, p, away, b, rs_sib[k, p, away, b])
            scatter(7 * k + 1 + p, pbuf.at[k, c, p, away], rs_sec.at[k, p], seconds[p])
        for p in halves:
            for b in (0, 1):
                add(k, p, a_me[p], b, rs_sib[k, p, a_me[p], b])

    def r2(k):
        if k < 0:
            return
        for p in halves:
            summed(7 * k + 1 + p, rs_sec.at[k, p], seconds[p])
            away = 1 - b_me[p]
            add(k, p, a_me[p], away, rs_sec[k, p, away])
            scatter(7 * k + 3 + p, pbuf.at[k, c, p, a_me[p], away], rs_fst.at[k, p], firsts[p])

    def r3(k):
        if k < 0:
            return
        for p in halves:
            summed(7 * k + 3 + p, rs_fst.at[k, p], firsts[p])
            total = (
                pbuf[k, c, p, a_me[p], b_me[p]].astype(F32)
                + rs_sec[k, p, b_me[p]].astype(F32)
                + rs_fst[k, p].astype(F32)
            )
            if k:
                pbuf[k, c, p, a_me[p], b_me[p]] = total.astype(BF16)
                mine = pbuf.at[k, c, p, a_me[p], b_me[p]]
                scatter(7 * k + 5 + p, mine, rs_z.at[k - 1, p], line[k])
            else:
                own_sum[p] = total

    def weight_columns(k):
        for xx in range(2):
            part = wt[k, xx]
            sub = lax.broadcasted_iota(jnp.int32, part.shape, 0)
            for s in range(slots):
                row = jnp.sum(jnp.where(sub == e * slots + s, part, 0.0), axis=0, keepdims=True)
                column = jnp.transpose(jnp.broadcast_to(row, (128, 128)))
                wcol[s, xx * rows : (xx + 1) * rows, :] = column[:rows]

    def up_gate(k, s):
        @pl.loop(0, tiles)
        def _(j):
            acc = jnp.zeros((2 * rows, 256), F32)
            for q in range(buf.shape[1]):
                acc = acc + jnp.dot(
                    buf[k, q], wgu[s * tiles + j, q * cols : (q + 1) * cols, :],
                    preferred_element_type=F32,
                )
            gate_out, up_out = acc[:, :128], acc[:, 128:]
            value = gate_out / (1.0 + jnp.exp(-gate_out)) * up_out * wcol[s]
            hid[:, pl.ds(pl.multiple_of(s * ff + j * 128, 128), 128)] = value.astype(BF16)

    def down(k):
        for q in range(buf.shape[1]):
            out = jnp.dot(hid[...], wd[:, q * cols : (q + 1) * cols], preferred_element_type=F32)
            out = out.astype(BF16)
            yy, cc = q // 2, q % 2
            for p in halves:
                for xx in range(2):
                    a, b = (yy, xx) if p == 0 else (xx, yy)
                    pbuf[k, cc, p, a, b] = out[
                        xx * rows : (xx + 1) * rows, p * half : (p + 1) * half
                    ]

    pl.semaphore_wait(barrier, len(peers))
    loads[0].wait()
    own = block(0, (y, x), c)
    along = [
        remote(own, block(k, (y, x), c), ag_send, ag_recv, k - 1, line[k]) for k in (1, 2, 3)
    ]
    along[0].start()
    a0(0)
    tags = [(line[1], 1, 0), (line[2], 2, 1), (line[3], 3, 2)]
    tags += [(cross[k], k, 3 + k) for k in range(4)]
    for peer, k, i in tags:
        send(wt.at[0, x], wt.at[k, x], wt_send, wt_recv, i, peer)
    for s in range(slots):
        for j in range(tiles):
            span = pl.ds(j * 128, 128)
            load(gate_ref.at[s, :, span], wgu.at[s * tiles + j, :, pl.ds(0, 128)])
            load(up_ref.at[s, :, span], wgu.at[s * tiles + j, :, pl.ds(128, 128)])
    for s in range(slots):
        load(down_ref.at[s], wd.at[pl.ds(s * ff, ff), :])
    a1(0)
    along[0].wait_send()
    along[1].start()
    a0(1)
    a2(0)
    a1(1)
    for peer, k, i in tags:
        got = wt.at[k, x if i < 3 else 1 - x]
        remote(got, got, wt_send, wt_recv, i, peer).wait_recv()
    for copy in loads[1:]:
        copy.wait()
    a3(0)
    for k in range(4):
        weight_columns(k)
        up_gate(k, 0)
        if k == 0:
            along[1].wait_send()
            along[2].start()
            started.append(along[2])
        r1(k - 1)
        r3(k - 2)
        a2(k + 1)
        a0(k + 2)
        up_gate(k, 1)
        a1(k + 2)
        down(k)
        r0(k)
        r2(k - 1)
        a3(k + 1)
    r1(3)
    r3(2)
    r2(3)
    r3(3)
    for p in halves:
        total = own_sum[p]
        for k in (1, 2, 3):
            summed(7 * k + 5 + p, rs_z.at[k - 1, p], line[k])
            total = total + rs_z[k - 1, p].astype(F32)
        out_ref[:, p * half : (p + 1) * half] = total.astype(BF16)
    for copy in started:
        copy.wait_send()


def fused_device(tokens, gate_weight, up_weight, down_weight, swap_slot, expert_ids, gate_fixed):
    rows, cols = tokens.shape
    slots, width, ff = gate_weight.shape
    quarters, half = width // cols, cols // 2
    chunks = 4
    scratch = [
        pltpu.VMEM((chunks, quarters, 2 * rows, cols), BF16),
        pltpu.VMEM((slots * ff // 128, width, 256), BF16),
        pltpu.VMEM((slots * ff, width), BF16),
        pltpu.VMEM((2 * rows, slots * ff), BF16),
        pltpu.VMEM((slots, 2 * rows, 128), F32),
        pltpu.VMEM((chunks, 2, 2, 2, 2, rows, half), BF16),
        pltpu.VMEM((chunks, 2, 16, 128), F32),
        pltpu.VMEM((chunks, 2, 2, 2, rows, half), BF16),
        pltpu.VMEM((chunks, 2, 2, rows, half), BF16),
        pltpu.VMEM((chunks, 2, rows, half), BF16),
        pltpu.VMEM((chunks - 1, 2, rows, half), BF16),
        pltpu.VMEM((2, rows, half), F32),
        pltpu.SemaphoreType.DMA((1 + 2 * slots * (ff // 128) + slots,)),
        pltpu.SemaphoreType.DMA((3 + 13 * chunks,)),
        pltpu.SemaphoreType.DMA((3 + 13 * chunks,)),
        pltpu.SemaphoreType.DMA((7,)),
        pltpu.SemaphoreType.DMA((7,)),
        pltpu.SemaphoreType.DMA((7 * chunks,)),
        pltpu.SemaphoreType.DMA((7 * chunks,)),
    ]
    any_space = pl.BlockSpec(memory_space=pl.ANY)
    vmem = pl.BlockSpec(memory_space=pltpu.VMEM)
    return pl.pallas_call(
        fused_kernel,
        out_shape=jax.ShapeDtypeStruct((rows, cols), BF16),
        in_specs=[any_space] * 4 + [vmem, vmem, pl.BlockSpec(memory_space=pltpu.SMEM)],
        out_specs=vmem,
        scratch_shapes=scratch,
        compiler_params=pltpu.CompilerParams(
            collective_id=0, has_side_effects=True, vmem_limit_bytes=56 * 1024 * 1024
        ),
    )(tokens, gate_weight, up_weight, down_weight, expert_ids.T, gate_fixed.T, swap_slot)


def per_device(tokens, *rest):
    small = lax.axis_size("expert") == 8 and lax.axis_size("hidden") == 4
    fits = tokens.shape == (96, 1024) and rest[0].shape == (2, 4096, 384)
    return fused_device(tokens, *rest) if small and fits else dense_device(tokens, *rest)


def solution(mesh):
    in_specs = (
        P("expert", "hidden"),
        P("expert", None, "hidden"),
        P("expert", None, "hidden"),
        P("expert", "hidden", None),
        P(),
        P("expert", None),
        P("expert", None),
    )
    return jax.shard_map(
        per_device, mesh=mesh, in_specs=in_specs, out_specs=P("expert", "hidden"), check_vma=False
    )
```
